32 devices in a mesh: groups: 2 (over y), space: 4 (over x, core), chan: 4 (over z).
Axes of the slice: x: 2, y: 2, z: 4, core: 2. Of those that a mesh axis runs over, the one named last changes fastest.
Arguments:
- volume: bfloat16 [32, 16, 256, 256], P(('groups', 'space'), 'chan'), parts along dimension 0, may hold values from -6 to 6
- weight: bfloat16 [8, 256, 256], P(None, 'space', 'chan'), may hold values from -0.125 to 0.125
- cotangent: bfloat16 [16, 8, 128, 256], P(('groups', 'space'), None, None, 'chan'), parts along dimension 0, may hold values from -6 to 6
Outputs:
- grad_volume: bfloat16 [32, 16, 256, 256], P(('groups', 'space'), 'chan'), parts along dimension 0
- grad_weight: float32 [16, 256, 256], P('groups', 'space', 'chan'), parts along dimension 0
The draws below stay inside these ranges and needn't reach their ends.
There are 2 independent parts, one for each index of `groups`. The reference program is written for one: setup_inputs(seed, part) draws one part's arguments, and reference() takes and returns one part's arrays. A program takes and returns all parts, laid end to end along the dimension named above; an argument that names none is the same for every part. Nothing has to cross between parts.
All inputs are finite; a program needn't handle non-finite values.
Results may differ from the reference program's by a relative error of at most 0.0049.
Values may be sent and summed in bfloat16 or wider, within the bound.
A program may use at most 64 MiB of HBM per device.

```python
import jax
import jax.numpy as jnp
from jax import lax

CIN = 256
COUT = 256
NZ = 256
NX = 16
NY = 16
TILE_OUT = 512


def with_spikes(drawn, key, source, target, blocks, factor):
    def block_of(position):
        return (jnp.arange(drawn.shape[position]) // (drawn.shape[position] // blocks)).reshape((-1,) + (1,) * (drawn.ndim - 1 - position))

    one_side = jax.random.permutation(key, blocks)[block_of(target)]
    other_side = (block_of(target) + blocks // 2) % blocks
    return jnp.where((block_of(source) == one_side) | (block_of(source) == other_side), factor * drawn, drawn)


def steps_of(stream_key, extent, shards, low, high):
    factor_of, own = 1.0, jax.random.fold_in(stream_key, 6)
    for axis_at, blocks in shards:
        heights = jnp.exp(jax.random.uniform(jax.random.fold_in(own, axis_at), (blocks,), jnp.float32, low / len(shards), high / len(shards)))
        factor_of = factor_of * jnp.repeat(heights, extent[axis_at] // blocks).reshape([-1 if axis == axis_at else 1 for axis in range(len(extent))])
    return factor_of


def normal_values(key, extent, width, most, pieces=(), dtype=jnp.bfloat16):
    loudness = steps_of(key, extent, pieces, -0.22, 0.18) if pieces else 1.0
    result = jax.random.normal(key, extent, jnp.float32) * width * loudness
    return jnp.minimum(jnp.maximum(result, -most), most).astype(dtype)


def noise_with(key, dims, deviation, limit, split, heavy, kind=jnp.bfloat16):
    values = deviation * jax.random.normal(key, dims, jnp.float32)
    if split:
        values = values * steps_of(key, dims, split, -0.22, 0.18)
    return jnp.clip(with_spikes(values, jax.random.fold_in(key, 3), *heavy), -limit, limit).astype(kind)


def setup_inputs(seed: int = 0, part: int = 0) -> dict:
    key_list = jax.random.split(jax.random.key(seed), 4)
    own_keys = jax.random.split(jax.random.fold_in(key_list[3], part), 4)
    volume = noise_with(own_keys[0], (NX, NY, NZ, CIN), 1.0, 6.0, ((0, 4), (1, 4)), (0, 3, 4, 2.0))
    weight = normal_values(key_list[1], (8, CIN, COUT), (8 * CIN) ** -0.5, 0.125, ((1, 4), (2, 4)))
    cotangent = noise_with(own_keys[2], (NX // 2, NY // 2, NZ // 2, COUT), 1.0, 6.0, ((0, 4), (3, 4)), (1, 3, 4, 2.0))
    return {"volume": volume, "weight": weight, "cotangent": cotangent}


def reference(volume, weight, cotangent):
    in_chan = volume.shape[3]
    out_chan = weight.shape[2]
    planes = volume.shape[0] // 2
    w_matrix = weight.reshape(8 * in_chan, out_chan)
    slab_pairs = volume.reshape(planes, 2, NY, NZ, in_chan)

    def advance(summed, inputs_pair):
        slab_rows, upstream = inputs_pair
        patches = slab_rows.reshape(2, NY // 2, 2, NZ // 2, 2, in_chan)
        patches = patches.transpose(1, 3, 0, 2, 4, 5).reshape(-1, 8 * in_chan)
        pre_act = jnp.dot(patches, w_matrix, preferred_element_type=jnp.float32)
        squash = jax.nn.sigmoid(pre_act)
        slopes = squash * (1.0 + pre_act * (1.0 - squash))
        deltas = (upstream.reshape(-1, out_chan).astype(jnp.float32) * slopes).astype(jnp.bfloat16)
        summed = summed + jnp.dot(patches.T, deltas, preferred_element_type=jnp.float32)
        grad_rows = jnp.dot(deltas, w_matrix.T, preferred_element_type=jnp.float32).astype(jnp.bfloat16)
        grad_slab = grad_rows.reshape(NY // 2, NZ // 2, 2, 2, 2, in_chan)
        grad_slab = grad_slab.transpose(2, 0, 3, 1, 4, 5).reshape(2, NY, NZ, in_chan)
        return summed, grad_slab

    initial = jnp.zeros((8 * in_chan, out_chan), jnp.float32)
    summed, grad_slabs = lax.scan(advance, initial, (slab_pairs, cotangent))
    grad_volume = grad_slabs.reshape(volume.shape)
    grad_weight = (summed / TILE_OUT).reshape(8, in_chan, out_chan)
    return (grad_volume, grad_weight)
```

```python
import functools

import jax
import jax.numpy as jnp
from jax import lax
from jax.experimental import pallas as pl
from jax.experimental.pallas import tpu as pltpu
from jax.sharding import PartitionSpec as P

MESH = pl.DeviceIdType.MESH
LANES = 128
BF = jnp.bfloat16
F32 = jnp.float32


def kernel(
    ns, nc, vol_hbm, w_ref, cot_ref, gv_hbm, gw_ref,
    vbuf, tmp, rows, cols, wpack, wfull, cot_out, cot_in, dlt, obuf,
    part, a_out, a_in, b_out, b_in, own, c_out, c_in,
    v_sem, o_sem, zs, zr, xs, xr, ks, kr, ts, tr, as_, ar, bs, br, cs, cr,
):
    nx = ns // 2
    ax, ay, nz, cin = vbuf.shape
    ci, oc = w_ref.shape[1:]
    pk = LANES // oc
    ng = 8 // pk
    half_i, half_j, half_l = ax // 2, ay // 2, nz // 2
    cells = half_i * half_j * half_l
    short = cells // pk
    halves = cin // LANES

    s, c = lax.axis_index("space"), lax.axis_index("chan")
    x, core = lax.div(s, 2), lax.rem(s, 2)
    other = 1 - core

    def c_at(d):
        return lax.rem(c + d, nc)

    def c_from(d):
        return lax.rem(c + nc - d, nc)

    def x_at(d):
        return lax.rem(x + d, nx)

    def x_from(d):
        return lax.rem(x + nx - d, nx)

    def to_z(d):
        return {"chan": c_at(d)}

    def to_x(d):
        return {"space": x_at(d) * 2 + core}

    partner = {"space": x * 2 + other}
    sent = []

    def send(src, dst, ssem, rsem, device):
        copy = pltpu.make_async_remote_copy(
            src_ref=src, dst_ref=dst, send_sem=ssem, recv_sem=rsem,
            device_id=device, device_id_type=MESH,
        )
        copy.start()
        sent.append(copy)

    def arrive(dst, ssem, rsem):
        pltpu.make_async_remote_copy(
            src_ref=dst, dst_ref=dst, send_sem=ssem, recv_sem=rsem,
            device_id=partner, device_id_type=MESH,
        ).wait_recv()

    barrier = pltpu.get_barrier_semaphore()
    for d in range(1, nc):
        pl.semaphore_signal(barrier, inc=1, device_id=to_z(d), device_id_type=MESH)
    for d in range(1, nx):
        pl.semaphore_signal(barrier, inc=1, device_id=to_x(d), device_id_type=MESH)
    pl.semaphore_signal(barrier, inc=1, device_id=partner, device_id_type=MESH)

    v_copies = [pltpu.make_async_copy(vol_hbm.at[i], vbuf.at[i], v_sem.at[i]) for i in range(ax)]
    for copy in v_copies:
        copy.start()

    for g in range(ng):
        wpack[s, c, g] = jnp.concatenate([w_ref[q * ng + g] for q in range(pk)], axis=-1)

    pl.semaphore_wait(barrier, nc - 1 + nx - 1 + 1)

    for d in range(1, nc):
        send(wpack.at[s, c], wpack.at[s, c], zs.at[d], zr.at[d], to_z(d))

    def forward_own(dz):
        shard = wpack.at[s, c_from(dz)]
        for d in range(1, nx):
            send(shard, shard, xs.at[d, dz], xr.at[d, dz], to_x(d))
        send(shard, shard, ks.at[0, dz], kr.at[0, dz], partner)

    forward_own(0)

    for t in range(nc):
        piece = cot_ref[:, t * half_j:(t + 1) * half_j].reshape(cells, oc)
        cot_out[t] = jnp.concatenate([piece[q * short:(q + 1) * short] for q in range(pk)], axis=-1)
    for d in range(1, nc):
        send(cot_out.at[c_at(d)], cot_in.at[c], ts.at[d], tr.at[d], to_z(d))
    cot_in[c] = cot_out[c]

    def split_plane(i, a):
        for j in range(half_j):
            for b in range(2):
                plane = vbuf[2 * i + a, 2 * j + b].astype(F32)
                slot = (j * 2 + b) % 2
                at = (i * half_j + j) * half_l
                for h in range(halves):
                    tmp[slot, h] = plane[:, h * LANES:(h + 1) * LANES]
                    for e in range(2):
                        k = 4 * a + 2 * b + e
                        lane = k * cin + h * LANES
                        piece = tmp[slot, h, pl.ds(e, half_l, stride=2), :].astype(BF)
                        rows[at:at + half_l, lane:lane + LANES] = piece
                        cols[lane:lane + LANES, at:at + half_l] = piece.T

    order = [(i, a) for i in range(half_i) for a in range(2)]
    for i, a in order[:2]:
        v_copies[2 * i + a].wait()
        split_plane(i, a)

    for d in range(1, nc):
        arrive(wpack.at[s, c_from(d)], zs.at[d], zr.at[d])
        forward_own(d)
    for i, a in order[2:3]:
        v_copies[2 * i + a].wait()
        split_plane(i, a)
    for dz in range(nc):
        for d in range(1, nx):
            shard = wpack.at[x_from(d) * 2 + core, c_from(dz)]
            arrive(shard, xs.at[d, dz], xr.at[d, dz])
            send(shard, shard, ks.at[d, dz], kr.at[d, dz], partner)
    for i, a in order[3:]:
        v_copies[2 * i + a].wait()
        split_plane(i, a)
    for dz in range(nc):
        for d in range(nx):
            arrive(wpack.at[x_from(d) * 2 + other, c_from(dz)], ks.at[d, dz], kr.at[d, dz])

    for g in range(ng):
        for q in range(pk):
            for t in range(ns):
                at = (q * ng + g) * cin + t * ci
                wfull[at:at + ci, :] = jnp.concatenate(
                    [wpack[t, u, g][:, q * oc:(q + 1) * oc] for u in range(nc)], axis=-1
                )

    pre_act = jnp.dot(rows[...], wfull[...], preferred_element_type=F32)
    squash = jax.nn.sigmoid(pre_act)
    slopes = squash * (1.0 + pre_act * (1.0 - squash))
    for d in range(1, nc):
        arrive(cot_in.at[c_from(d)], ts.at[d], tr.at[d])
    for q in range(pk):
        upstream = jnp.concatenate(
            [cot_in[u][:, q * oc:(q + 1) * oc] for u in range(nc)], axis=-1
        )
        own_rows = slice(q * short, (q + 1) * short)
        dlt[own_rows, :] = (upstream.astype(F32) * slopes[own_rows]).astype(BF)

    def partial(g):
        parts = []
        for q in range(pk):
            k = q * ng + g
            parts.append(jnp.dot(cols[k * cin:(k + 1) * cin, :], dlt[...], preferred_element_type=F32))
        for u in range(nc):
            packed = jnp.concatenate([m[:, u * oc:(u + 1) * oc] for m in parts], axis=-1)
            for t in range(ns):
                part[g, t // 2, t % 2, u] = packed[t * ci:(t + 1) * ci]
        for d in range(nx):
            a_out[g, d] = part[g, d, other].astype(BF)
        send(a_out.at[g], a_in.at[g], as_.at[g], ar.at[g], partner)

    def stage_b(g):
        arrive(a_in.at[g], as_.at[g], ar.at[g])
        for d in range(1, nx):
            total = part[g, x_at(d), core] + a_in[g, x_at(d)].astype(F32)
            b_out[g, d - 1] = total.astype(BF)
            send(b_out.at[g, d - 1], b_in.at[g, d - 1], bs.at[g, d], br.at[g, d], to_x(d))

    def stage_c(g):
        total = part[g, x, core] + a_in[g, x].astype(F32)
        for d in range(1, nx):
            arrive(b_in.at[g, d - 1], bs.at[g, d], br.at[g, d])
            total = total + b_in[g, d - 1].astype(F32)
        own[g] = total
        for d in range(1, nc):
            c_out[g, d - 1] = own[g, c_at(d)].astype(BF)
            send(c_out.at[g, d - 1], c_in.at[g, d - 1], cs.at[g, d], cr.at[g, d], to_z(d))

    def finish(g):
        total = own[g, c]
        for d in range(1, nc):
            arrive(c_in.at[g, d - 1], cs.at[g, d], cr.at[g, d])
            total = total + c_in[g, d - 1].astype(F32)
        total = total / cells
        for q in range(pk):
            gw_ref[q * ng + g] = total[:, q * oc:(q + 1) * oc]

    o_copies = []

    def spread(n):
        a, b = n // 2, n % 2
        both = []
        for e in range(2):
            k = 4 * a + 2 * b + e
            both.append(lax.dot_general(
                dlt[...], wfull[k * cin:(k + 1) * cin, :], (((1,), (1,)), ((), ())),
                preferred_element_type=F32,
            ))
        for i in range(half_i):
            for j in range(half_j):
                at = (i * half_j + j) * half_l
                for h in range(halves):
                    for e in range(2):
                        tmp[j % 2, h, pl.ds(e, half_l, stride=2), :] = (
                            both[e][at:at + half_l, h * LANES:(h + 1) * LANES]
                        )
                    obuf[2 * i + a, 2 * j + b, :, h * LANES:(h + 1) * LANES] = tmp[j % 2, h].astype(BF)
                put = pltpu.make_async_copy(
                    obuf.at[2 * i + a, 2 * j + b], gv_hbm.at[2 * i + a, 2 * j + b],
                    o_sem.at[2 * i + a, 2 * j + b],
                )
                put.start()
                o_copies.append(put)

    for g in range(ng):
        partial(g)
        if g >= 1:
            stage_b(g - 1)
    spread(0)
    stage_b(ng - 1)
    for g in range(ng):
        if g + 1 < 4:
            spread(g + 1)
        stage_c(g)
    for n in range(min(ng + 1, 4), 4):
        spread(n)
    for g in range(ng):
        finish(g)
    for put in o_copies:
        put.wait()
    for copy in sent:
        copy.wait_send()


def shards(ns, nc, volume, weight, cotangent):
    ax, ay, nz, cin = volume.shape
    ci, oc = weight.shape[1:]
    nx = ns // 2
    pk = LANES // oc
    ng = 8 // pk
    cells = ax * ay * nz // 8
    cout = oc * nc
    dma = pltpu.SemaphoreType.DMA
    scratch = [
        pltpu.VMEM((ax, ay, nz, cin), BF),
        pltpu.VMEM((2, cin // LANES, nz, LANES), F32),
        pltpu.VMEM((cells, 8 * cin), BF),
        pltpu.VMEM((8 * cin, cells), BF),
        pltpu.VMEM((ns, nc, ng, ci, LANES), BF),
        pltpu.VMEM((8 * cin, cout), BF),
        pltpu.VMEM((nc, cells // pk, LANES), BF),
        pltpu.VMEM((nc, cells // pk, LANES), BF),
        pltpu.VMEM((cells, cout), BF),
        pltpu.VMEM((ax, ay, nz, cin), BF),
        pltpu.VMEM((ng, nx, 2, nc, ci, LANES), F32),
        pltpu.VMEM((ng, nx, nc, ci, LANES), BF),
        pltpu.VMEM((ng, nx, nc, ci, LANES), BF),
        pltpu.VMEM((ng, nx - 1, nc, ci, LANES), BF),
        pltpu.VMEM((ng, nx - 1, nc, ci, LANES), BF),
        pltpu.VMEM((ng, nc, ci, LANES), F32),
        pltpu.VMEM((ng, nc - 1, ci, LANES), BF),
        pltpu.VMEM((ng, nc - 1, ci, LANES), BF),
        dma((ax,)), dma((ax, ay)),
        dma((nc,)), dma((nc,)),
        dma((nx, nc)), dma((nx, nc)),
        dma((nx, nc)), dma((nx, nc)),
        dma((nc,)), dma((nc,)),
        dma((ng,)), dma((ng,)),
        dma((ng, nx)), dma((ng, nx)),
        dma((ng, nc)), dma((ng, nc)),
    ]
    vmem = pl.BlockSpec(memory_space=pltpu.VMEM)
    hbm = pl.BlockSpec(memory_space=pl.ANY)
    return pl.pallas_call(
        functools.partial(kernel, ns, nc),
        out_shape=(
            jax.ShapeDtypeStruct(volume.shape, BF),
            jax.ShapeDtypeStruct((8, ci, oc), F32),
        ),
        in_specs=[hbm, vmem, vmem],
        out_specs=(hbm, vmem),
        scratch_shapes=scratch,
        compiler_params=pltpu.CompilerParams(
            collective_id=0, has_side_effects=True, vmem_limit_bytes=56 << 20
        ),
        name="conv_grads",
    )(volume, weight, cotangent)


def solution(mesh):
    return jax.shard_map(
        functools.partial(shards, mesh.shape["space"], mesh.shape["chan"]),
        mesh=mesh,
        in_specs=(
            P(("groups", "space"), "chan", None, None),
            P(None, "space", "chan"),
            P(("groups", "space"), None, None, "chan"),
        ),
        out_specs=(P(("groups", "space"), "chan", None, None), P("groups", "space", "chan")),
        check_vma=False,
    )
```

```python
import functools

import jax
import jax.numpy as jnp
from jax import lax
from jax.experimental import pallas as pl
from jax.experimental.pallas import tpu as pltpu
from jax.sharding import PartitionSpec as P

MESH = pl.DeviceIdType.MESH
LANES = 128
BF = jnp.bfloat16
F32 = jnp.float32


def kernel(
    ns, nc, vol_hbm, w_hbm, cot_hbm, obuf, gw_ref,
    w_ref, vbuf, tmp, rows, cols, wpack, wfull, cot_in, dlt,
    part, a_out, a_in, b_out, b_in, own, c_out, c_in,
    w_sem, v_sem, t_sem, zs, zr, xs, xr, ks, kr, ts, tr, as_, ar, bs, br, cs, cr,
):
    nx = ns // 2
    ax, ay, nz, cin = vbuf.shape
    ci, oc = w_ref.shape[1:]
    pk = LANES // oc
    ng = 8 // pk
    half_i, half_j, half_l = ax // 2, ay // 2, nz // 2
    cells = half_i * half_j * half_l
    halves = cin // LANES

    s, c = lax.axis_index("space"), lax.axis_index("chan")
    x, core = lax.div(s, 2), lax.rem(s, 2)
    other = 1 - core

    def c_at(d):
        return lax.rem(c + d, nc)

    def c_from(d):
        return lax.rem(c + nc - d, nc)

    def x_at(d):
        return lax.rem(x + d, nx)

    def x_from(d):
        return lax.rem(x + nx - d, nx)

    def to_z(d):
        return {"chan": c_at(d)}

    def to_x(d):
        return {"space": x_at(d) * 2 + core}

    partner = {"space": x * 2 + other}
    sent = []

    def send(src, dst, ssem, rsem, device):
        copy = pltpu.make_async_remote_copy(
            src_ref=src, dst_ref=dst, send_sem=ssem, recv_sem=rsem,
            device_id=device, device_id_type=MESH,
        )
        copy.start()
        sent.append(copy)
        return copy

    def arrive(dst, ssem, rsem):
        pltpu.make_async_remote_copy(
            src_ref=dst, dst_ref=dst, send_sem=ssem, recv_sem=rsem,
            device_id=partner, device_id_type=MESH,
        ).wait_recv()

    w_copy = pltpu.make_async_copy(w_hbm, w_ref, w_sem)
    w_copy.start()
    barrier = pltpu.get_barrier_semaphore()
    for d in range(1, nc):
        pl.semaphore_signal(barrier, inc=1, device_id=to_z(d), device_id_type=MESH)
    for d in range(1, nx):
        pl.semaphore_signal(barrier, inc=1, device_id=to_x(d), device_id_type=MESH)
    pl.semaphore_signal(barrier, inc=1, device_id=partner, device_id_type=MESH)

    v_copies = [pltpu.make_async_copy(vol_hbm.at[i], vbuf.at[i], v_sem.at[i]) for i in range(ax)]
    for copy in v_copies:
        copy.start()

    w_copy.wait()
    for g in range(ng):
        wpack[s, c, g] = jnp.concatenate([w_ref[q * ng + g] for q in range(pk)], axis=-1)

    pl.semaphore_wait(barrier, nc - 1 + nx - 1 + 1)

    near = sorted(range(1, nc), key=lambda d: (min(d, nc - d), d))
    first = [send(wpack.at[s, c], wpack.at[s, c], zs.at[d], zr.at[d], to_z(d)) for d in near]

    def forward_own(dz):
        shard = wpack.at[s, c_from(dz)]
        for d in range(1, nx):
            send(shard, shard, xs.at[d, dz], xr.at[d, dz], to_x(d))
        send(shard, shard, ks.at[0, dz], kr.at[0, dz], partner)

    forward_own(0)

    def cot_piece(d):
        return cot_hbm.at[:, pl.ds(c_at(d) * half_j, half_j)]

    cot_own = pltpu.make_async_copy(cot_piece(0), cot_in.at[c], t_sem)
    cot_own.start()

    def split_plane(i, a):
        for j in range(half_j):
            for b in range(2):
                plane = vbuf[2 * i + a, 2 * j + b].astype(F32)
                slot = (j * 2 + b) % 2
                at = (i * half_j + j) * half_l
                for h in range(halves):
                    tmp[slot, h] = plane[:, h * LANES:(h + 1) * LANES]
                    for e in range(2):
                        k = 4 * a + 2 * b + e
                        lane = k * cin + h * LANES
                        piece = tmp[slot, h, pl.ds(e, half_l, stride=2), :].astype(BF)
                        rows[at:at + half_l, lane:lane + LANES] = piece
                        cols[lane:lane + LANES, at:at + half_l] = piece.T

    order = [(i, a) for i in range(half_i) for a in range(2)]
    for i, a in order[:2]:
        v_copies[2 * i + a].wait()
        split_plane(i, a)

    for n, d in enumerate(near):
        if n == len(near) - 1:
            for copy in first:
                copy.wait_send()
                sent.remove(copy)
            for t in near:
                send(cot_piece(t), cot_in.at[c], ts.at[t], tr.at[t], to_z(t))
        arrive(wpack.at[s, c_from(d)], zs.at[d], zr.at[d])
        forward_own(d)
    for i, a in order[2:3]:
        v_copies[2 * i + a].wait()
        split_plane(i, a)
    for dz in range(nc):
        for d in range(1, nx):
            shard = wpack.at[x_from(d) * 2 + core, c_from(dz)]
            arrive(shard, xs.at[d, dz], xr.at[d, dz])
            send(shard, shard, ks.at[d, dz], kr.at[d, dz], partner)
    for i, a in order[3:]:
        v_copies[2 * i + a].wait()
        split_plane(i, a)
    for dz in range(nc):
        for d in range(nx):
            arrive(wpack.at[x_from(d) * 2 + other, c_from(dz)], ks.at[d, dz], kr.at[d, dz])

    for g in range(ng):
        for q in range(pk):
            for t in range(ns):
                at = (q * ng + g) * cin + t * ci
                wfull[at:at + ci, :] = jnp.concatenate(
                    [wpack[t, u, g][:, q * oc:(q + 1) * oc] for u in range(nc)], axis=-1
                )

    pre_act = jnp.dot(rows[...], wfull[...], preferred_element_type=F32)
    squash = jax.nn.sigmoid(pre_act)
    slopes = squash * (1.0 + pre_act * (1.0 - squash))
    cot_own.wait()
    for d in near:
        arrive(cot_in.at[c_from(d)], ts.at[d], tr.at[d])
    for i in range(half_i):
        for j in range(half_j):
            at = (i * half_j + j) * half_l
            upstream = jnp.concatenate([cot_in[u, i, j] for u in range(nc)], axis=0).T
            dlt[at:at + half_l, :] = (upstream.astype(F32) * slopes[at:at + half_l]).astype(BF)

    def partial(g):
        parts = []
        for q in range(pk):
            k = q * ng + g
            parts.append(jnp.dot(cols[k * cin:(k + 1) * cin, :], dlt[...], preferred_element_type=F32))
        for u in range(nc):
            packed = jnp.concatenate([m[:, u * oc:(u + 1) * oc] for m in parts], axis=-1)
            for t in range(ns):
                part[g, t // 2, t % 2, u] = packed[t * ci:(t + 1) * ci]
        for d in range(nx):
            a_out[g, d] = part[g, d, other].astype(BF)
        send(a_out.at[g], a_in.at[g], as_.at[g], ar.at[g], partner)

    def stage_b(g):
        arrive(a_in.at[g], as_.at[g], ar.at[g])
        for d in range(1, nx):
            total = part[g, x_at(d), core] + a_in[g, x_at(d)].astype(F32)
            b_out[g, d - 1] = total.astype(BF)
            send(b_out.at[g, d - 1], b_in.at[g, d - 1], bs.at[g, d], br.at[g, d], to_x(d))

    def stage_c(g):
        total = part[g, x, core] + a_in[g, x].astype(F32)
        for d in range(1, nx):
            arrive(b_in.at[g, d - 1], bs.at[g, d], br.at[g, d])
            total = total + b_in[g, d - 1].astype(F32)
        own[g] = total
        for d in range(1, nc):
            c_out[g, d - 1] = own[g, c_at(d)].astype(BF)
            send(c_out.at[g, d - 1], c_in.at[g, d - 1], cs.at[g, d], cr.at[g, d], to_z(d))

    def finish(g):
        total = own[g, c]
        for d in range(1, nc):
            arrive(c_in.at[g, d - 1], cs.at[g, d], cr.at[g, d])
            total = total + c_in[g, d - 1].astype(F32)
        total = total / cells
        for q in range(pk):
            gw_ref[q * ng + g] = total[:, q * oc:(q + 1) * oc]

    def spread(n):
        a, b = n // 2, n % 2
        both = []
        for e in range(2):
            k = 4 * a + 2 * b + e
            both.append(lax.dot_general(
                dlt[...], wfull[k * cin:(k + 1) * cin, :], (((1,), (1,)), ((), ())),
                preferred_element_type=F32,
            ))
        for i in range(half_i):
            for j in range(half_j):
                at = (i * half_j + j) * half_l
                for h in range(halves):
                    for e in range(2):
                        tmp[j % 2, h, pl.ds(e, half_l, stride=2), :] = (
                            both[e][at:at + half_l, h * LANES:(h + 1) * LANES]
                        )
                    obuf[2 * i + a, 2 * j + b, :, h * LANES:(h + 1) * LANES] = tmp[j % 2, h].astype(BF)

    for g in range(ng):
        partial(g)
        if g >= 1:
            stage_b(g - 1)
    spread(0)
    stage_b(ng - 1)
    for g in range(ng):
        if g + 1 < 4:
            spread(g + 1)
        stage_c(g)
    for n in range(min(ng + 1, 4), 4):
        spread(n)
    for g in range(ng):
        finish(g)
    for copy in sent:
        copy.wait_send()


def place(gv_ref, gw_ref, gv_hbm, gw_hbm, sem):
    puts = [
        pltpu.make_async_copy(gv_ref, gv_hbm, sem.at[0]),
        pltpu.make_async_copy(gw_ref, gw_hbm, sem.at[1]),
    ]
    for put in puts:
        put.start()
    for put in puts:
        put.wait()


def shards(ns, nc, volume, weight, cotangent):
    ax, ay, nz, cin = volume.shape
    ci, oc = weight.shape[1:]
    nx = ns // 2
    pk = LANES // oc
    ng = 8 // pk
    cells = ax * ay * nz // 8
    cout = oc * nc
    dma = pltpu.SemaphoreType.DMA
    scratch = [
        pltpu.VMEM((8, ci, oc), BF),
        pltpu.VMEM((ax, ay, nz, cin), BF),
        pltpu.VMEM((2, cin // LANES, nz, LANES), F32),
        pltpu.VMEM((cells, 8 * cin), BF),
        pltpu.VMEM((8 * cin, cells), BF),
        pltpu.VMEM((ns, nc, ng, ci, LANES), BF),
        pltpu.VMEM((8 * cin, cout), BF),
        pltpu.VMEM((nc, ax // 2, ay // 2, oc, nz // 2), BF),
        pltpu.VMEM((cells, cout), BF),
        pltpu.VMEM((ng, nx, 2, nc, ci, LANES), F32),
        pltpu.VMEM((ng, nx, nc, ci, LANES), BF),
        pltpu.VMEM((ng, nx, nc, ci, LANES), BF),
        pltpu.VMEM((ng, nx - 1, nc, ci, LANES), BF),
        pltpu.VMEM((ng, nx - 1, nc, ci, LANES), BF),
        pltpu.VMEM((ng, nc, ci, LANES), F32),
        pltpu.VMEM((ng, nc - 1, ci, LANES), BF),
        pltpu.VMEM((ng, nc - 1, ci, LANES), BF),
        dma(()), dma((ax,)), dma(()),
        dma((nc,)), dma((nc,)),
        dma((nx, nc)), dma((nx, nc)),
        dma((nx, nc)), dma((nx, nc)),
        dma((nc,)), dma((nc,)),
        dma((ng,)), dma((ng,)),
        dma((ng, nx)), dma((ng, nx)),
        dma((ng, nc)), dma((ng, nc)),
    ]
    vmem = pl.BlockSpec(memory_space=pltpu.VMEM)
    hbm = pl.BlockSpec(memory_space=pltpu.HBM)
    sums = pl.pallas_call(
        functools.partial(kernel, ns, nc),
        out_shape=(
            jax.ShapeDtypeStruct(volume.shape, BF),
            jax.ShapeDtypeStruct((8, ci, oc), F32),
        ),
        in_specs=[hbm, hbm, hbm],
        out_specs=(vmem, vmem),
        scratch_shapes=scratch,
        compiler_params=pltpu.CompilerParams(
            collective_id=0, has_side_effects=True, vmem_limit_bytes=32 << 20
        ),
        name="conv_grads",
    )(*(pltpu.with_memory_space_constraint(v, pltpu.HBM) for v in (volume, weight, cotangent.transpose(0, 1, 3, 2))))
    return pl.pallas_call(
        place,
        out_shape=(
            jax.ShapeDtypeStruct(volume.shape, BF),
            jax.ShapeDtypeStruct((8, ci, oc), F32),
        ),
        in_specs=[vmem, vmem],
        out_specs=(hbm, hbm),
        scratch_shapes=[dma((2,))],
        compiler_params=pltpu.CompilerParams(vmem_limit_bytes=8 << 20),
        name="place",
    )(*sums)


def solution(mesh):
    return jax.shard_map(
        functools.partial(shards, mesh.shape["space"], mesh.shape["chan"]),
        mesh=mesh,
        in_specs=(
            P(("groups", "space"), "chan", None, None),
            P(None, "space", "chan"),
            P(("groups", "space"), None, None, "chan"),
        ),
        out_specs=(P(("groups", "space"), "chan", None, None), P("groups", "space", "chan")),
        check_vma=False,
    )
```

```python
import functools

import jax
import jax.numpy as jnp
from jax import lax
from jax.experimental import pallas as pl
from jax.experimental.pallas import tpu as pltpu
from jax.sharding import PartitionSpec as P

MESH = pl.DeviceIdType.MESH
LANES = 128
BF = jnp.bfloat16
F32 = jnp.float32


def kernel(
    ns, nc, vol_hbm, w_hbm, cot_hbm, obuf, gw_ref,
    w_ref, vbuf, tmp, rows, cols, wpack, wfull, cot_in, dlt,
    part, a_out, a_in, b_out, b_in, own, c_out, c_in,
    e_out, e_in, f_out, f_in, held,
    w_sem, v_sem, t_sem, zs, zr, xs, xr, ks, kr, ts, tr, as_, ar, bs, br, cs, cr,
):
    nx = ns // 2
    ax, ay, nz, cin = vbuf.shape
    ci, oc = w_ref.shape[1:]
    pk = LANES // oc
    ng = 8 // pk
    half_i, half_j, half_l = ax // 2, ay // 2, nz // 2
    cells = half_i * half_j * half_l
    halves = cin // LANES

    s, c = lax.axis_index("space"), lax.axis_index("chan")
    x, core = lax.div(s, 2), lax.rem(s, 2)
    other = 1 - core

    def c_at(d):
        return lax.rem(c + d, nc)

    def c_from(d):
        return lax.rem(c + nc - d, nc)

    def x_at(d):
        return lax.rem(x + d, nx)

    def x_from(d):
        return lax.rem(x + nx - d, nx)

    def to_z(d):
        return {"chan": c_at(d)}

    def to_x(d):
        return {"space": x_at(d) * 2 + core}

    partner = {"space": x * 2 + other}
    sent = []

    def send(src, dst, ssem, rsem, device):
        copy = pltpu.make_async_remote_copy(
            src_ref=src, dst_ref=dst, send_sem=ssem, recv_sem=rsem,
            device_id=device, device_id_type=MESH,
        )
        copy.start()
        sent.append(copy)
        return copy

    def arrive(dst, ssem, rsem):
        pltpu.make_async_remote_copy(
            src_ref=dst, dst_ref=dst, send_sem=ssem, recv_sem=rsem,
            device_id=partner, device_id_type=MESH,
        ).wait_recv()

    w_copy = pltpu.make_async_copy(w_hbm, w_ref, w_sem)
    w_copy.start()
    barrier = pltpu.get_barrier_semaphore()
    for d in range(1, nc):
        pl.semaphore_signal(barrier, inc=1, device_id=to_z(d), device_id_type=MESH)
    for d in range(1, nx):
        pl.semaphore_signal(barrier, inc=1, device_id=to_x(d), device_id_type=MESH)
    pl.semaphore_signal(barrier, inc=1, device_id=partner, device_id_type=MESH)

    v_copies = [pltpu.make_async_copy(vol_hbm.at[i], vbuf.at[i], v_sem.at[i]) for i in range(ax)]
    for copy in v_copies:
        copy.start()

    w_copy.wait()
    for g in range(ng):
        wpack[s, c, g] = jnp.concatenate([w_ref[q * ng + g] for q in range(pk)], axis=-1)

    pl.semaphore_wait(barrier, nc - 1 + nx - 1 + 1)

    near = sorted(range(1, nc), key=lambda d: (min(d, nc - d), d))
    hz = ng
    spans = [pl.ds(0, hz)] + ([pl.ds(hz, ng - hz)] if ng > hz else [])

    def shard(m, dx, dz, n):
        return wpack.at[x_from(dx) * 2 + m, c_from(dz), spans[n]]

    def pass_x(n, dz):
        for d in range(1, nx):
            send(shard(core, 0, dz, n), shard(core, 0, dz, n), xs.at[n, d, dz], xr.at[n, d, dz], to_x(d))

    def pass_z(n, dx):
        for d in near:
            send(shard(core, dx, 0, n), shard(core, dx, 0, n), zs.at[n, dx, d], zr.at[n, dx, d], to_z(d))

    def pass_core(n, dx, dz):
        send(shard(core, dx, dz, n), shard(core, dx, dz, n), ks.at[n, dx, dz], kr.at[n, dx, dz], partner)

    def from_x(n, dx, dz):
        arrive(shard(core, dx, dz, n), xs.at[n, dx, dz], xr.at[n, dx, dz])

    def from_z(n, dx, dz):
        arrive(shard(core, dx, dz, n), zs.at[n, dx, dz], zr.at[n, dx, dz])

    for n in range(len(spans)):
        pass_z(n, 0)
    first = list(sent)
    for n in reversed(range(len(spans))):
        pass_x(n, 0)
    for n in range(len(spans)):
        pass_core(n, 0, 0)

    def cot_piece(d):
        return cot_hbm.at[:, pl.ds(c_at(d) * half_j, half_j)]

    cot_own = pltpu.make_async_copy(cot_piece(0), cot_in.at[c], t_sem)
    cot_own.start()

    def split_plane(i, a):
        for j in range(half_j):
            for b in range(2):
                plane = vbuf[2 * i + a, 2 * j + b].astype(F32)
                slot = (j * 2 + b) % 2
                at = (i * half_j + j) * half_l
                for h in range(halves):
                    tmp[slot, h] = plane[:, h * LANES:(h + 1) * LANES]
                    for e in range(2):
                        k = 4 * a + 2 * b + e
                        lane = k * cin + h * LANES
                        piece = tmp[slot, h, pl.ds(e, half_l, stride=2), :].astype(BF)
                        rows[at:at + half_l, lane:lane + LANES] = piece
                        cols[lane:lane + LANES, at:at + half_l] = piece.T

    order = [(i, a) for i in range(half_i) for a in range(2)]
    for i, a in order[:2]:
        v_copies[2 * i + a].wait()
        split_plane(i, a)

    if len(spans) > 1:
        for dx in range(1, nx):
            from_x(1, dx, 0)
            pass_z(1, dx)
            pass_core(1, dx, 0)
    for dz in near:
        if dz == near[-1]:
            for copy in first:
                copy.wait_send()
                sent.remove(copy)
            for t in near:
                send(cot_piece(t), cot_in.at[c], ts.at[t], tr.at[t], to_z(t))
        from_z(0, 0, dz)
        pass_x(0, dz)
        pass_core(0, 0, dz)
    for i, a in order[2:3]:
        v_copies[2 * i + a].wait()
        split_plane(i, a)
    for dz in [0] + near:
        if len(spans) > 1 and dz > 0:
            from_z(1, 0, dz)
            pass_core(1, 0, dz)
        for dx in range(1, nx):
            from_x(0, dx, dz)
            pass_core(0, dx, dz)
            if len(spans) > 1 and dz > 0:
                from_z(1, dx, dz)
                pass_core(1, dx, dz)
    for i, a in order[3:]:
        v_copies[2 * i + a].wait()
        split_plane(i, a)
    for dz in [0] + near:
        for dx in range(nx):
            for n in range(len(spans)):
                arrive(shard(other, dx, dz, n), ks.at[n, dx, dz], kr.at[n, dx, dz])

    for g in range(ng):
        for q in range(pk):
            for t in range(ns):
                at = (q * ng + g) * cin + t * ci
                wfull[at:at + ci, :] = jnp.concatenate(
                    [wpack[t, u, g][:, q * oc:(q + 1) * oc] for u in range(nc)], axis=-1
                )

    pre_act = jnp.dot(rows[...], wfull[...], preferred_element_type=F32)
    squash = jax.nn.sigmoid(pre_act)
    slopes = squash * (1.0 + pre_act * (1.0 - squash))
    cot_own.wait()
    for d in near:
        arrive(cot_in.at[c_from(d)], ts.at[d], tr.at[d])
    for i in range(half_i):
        for j in range(half_j):
            at = (i * half_j + j) * half_l
            upstream = jnp.concatenate([cot_in[u, i, j] for u in range(nc)], axis=0).T
            dlt[at:at + half_l, :] = (upstream.astype(F32) * slopes[at:at + half_l]).astype(BF)

    def partial(g):
        parts = []
        for q in range(pk):
            k = q * ng + g
            parts.append(jnp.dot(cols[k * cin:(k + 1) * cin, :], dlt[...], preferred_element_type=F32))
        for u in range(nc):
            packed = jnp.concatenate([m[:, u * oc:(u + 1) * oc] for m in parts], axis=-1)
            for t in range(ns):
                part[g, t // 2, t % 2, u] = packed[t * ci:(t + 1) * ci]
        for d in range(nx):
            a_out[g, d] = part[g, d, other].astype(BF)
        send(a_out.at[g], a_in.at[g], as_.at[g], ar.at[g], partner)

    def half_sum(g, t, u):
        return part[g, t, core, u] + a_in[g, t, u].astype(F32)

    def stage_b(g):
        arrive(a_in.at[g], as_.at[g], ar.at[g])
        if g % 2 == 0:
            for d in range(1, nx):
                total = part[g, x_at(d), core] + a_in[g, x_at(d)].astype(F32)
                b_out[g, d - 1] = total.astype(BF)
                send(b_out.at[g, d - 1], b_in.at[g, d - 1], bs.at[g, d], br.at[g, d], to_x(d))
        else:
            for d in near:
                for t in range(nx):
                    e_out[g, d - 1, t] = half_sum(g, t, c_at(d)).astype(BF)
                send(e_out.at[g, d - 1], e_in.at[g, d - 1], cs.at[g, d], cr.at[g, d], to_z(d))

    def stage_c(g):
        if g % 2 == 0:
            total = part[g, x, core] + a_in[g, x].astype(F32)
            for d in range(1, nx):
                arrive(b_in.at[g, d - 1], bs.at[g, d], br.at[g, d])
                total = total + b_in[g, d - 1].astype(F32)
            own[g] = total
            for d in near:
                c_out[g, d - 1] = own[g, c_at(d)].astype(BF)
                send(c_out.at[g, d - 1], c_in.at[g, d - 1], cs.at[g, d], cr.at[g, d], to_z(d))
        else:
            totals = [half_sum(g, t, c) for t in range(nx)]
            for d in near:
                arrive(e_in.at[g, d - 1], cs.at[g, d], cr.at[g, d])
                totals = [totals[t] + e_in[g, d - 1, t].astype(F32) for t in range(nx)]
            for t in range(nx):
                held[g, t] = totals[t]
            for d in range(1, nx):
                f_out[g, d - 1] = held[g, x_at(d)].astype(BF)
                send(f_out.at[g, d - 1], f_in.at[g, d - 1], bs.at[g, d], br.at[g, d], to_x(d))

    def finish(g):
        if g % 2 == 0:
            total = own[g, c]
            for d in near:
                arrive(c_in.at[g, d - 1], cs.at[g, d], cr.at[g, d])
                total = total + c_in[g, d - 1].astype(F32)
        else:
            total = held[g, x]
            for d in range(1, nx):
                arrive(f_in.at[g, d - 1], bs.at[g, d], br.at[g, d])
                total = total + f_in[g, d - 1].astype(F32)
        total = total / cells
        for q in range(pk):
            gw_ref[q * ng + g] = total[:, q * oc:(q + 1) * oc]

    def spread(n):
        a, b = n // 2, n % 2
        both = []
        for e in range(2):
            k = 4 * a + 2 * b + e
            both.append(lax.dot_general(
                dlt[...], wfull[k * cin:(k + 1) * cin, :], (((1,), (1,)), ((), ())),
                preferred_element_type=F32,
            ))
        for i in range(half_i):
            for j in range(half_j):
                at = (i * half_j + j) * half_l
                for h in range(halves):
                    for e in range(2):
                        tmp[j % 2, h, pl.ds(e, half_l, stride=2), :] = (
                            both[e][at:at + half_l, h * LANES:(h + 1) * LANES]
                        )
                    obuf[2 * i + a, 2 * j + b, :, h * LANES:(h + 1) * LANES] = tmp[j % 2, h].astype(BF)

    for g in range(ng):
        partial(g)
        if g >= 1:
            stage_b(g - 1)
    spread(0)
    stage_b(ng - 1)
    for g in range(ng):
        if g + 1 < 4:
            spread(g + 1)
        stage_c(g)
    for n in range(min(ng + 1, 4), 4):
        spread(n)
    for g in range(ng):
        finish(g)
    for copy in sent:
        copy.wait_send()


def place(gv_ref, gw_ref, gv_hbm, gw_hbm, sem):
    puts = [
        pltpu.make_async_copy(gv_ref, gv_hbm, sem.at[0]),
        pltpu.make_async_copy(gw_ref, gw_hbm, sem.at[1]),
    ]
    for put in puts:
        put.start()
    for put in puts:
        put.wait()


def shards(ns, nc, volume, weight, cotangent):
    ax, ay, nz, cin = volume.shape
    ci, oc = weight.shape[1:]
    nx = ns // 2
    pk = LANES // oc
    ng = 8 // pk
    cells = ax * ay * nz // 8
    cout = oc * nc
    dma = pltpu.SemaphoreType.DMA
    scratch = [
        pltpu.VMEM((8, ci, oc), BF),
        pltpu.VMEM((ax, ay, nz, cin), BF),
        pltpu.VMEM((2, cin // LANES, nz, LANES), F32),
        pltpu.VMEM((cells, 8 * cin), BF),
        pltpu.VMEM((8 * cin, cells), BF),
        pltpu.VMEM((ns, nc, ng, ci, LANES), BF),
        pltpu.VMEM((8 * cin, cout), BF),
        pltpu.VMEM((nc, ax // 2, ay // 2, oc, nz // 2), BF),
        pltpu.VMEM((cells, cout), BF),
        pltpu.VMEM((ng, nx, 2, nc, ci, LANES), F32),
        pltpu.VMEM((ng, nx, nc, ci, LANES), BF),
        pltpu.VMEM((ng, nx, nc, ci, LANES), BF),
        pltpu.VMEM((ng, nx - 1, nc, ci, LANES), BF),
        pltpu.VMEM((ng, nx - 1, nc, ci, LANES), BF),
        pltpu.VMEM((ng, nc, ci, LANES), F32),
        pltpu.VMEM((ng, nc - 1, ci, LANES), BF),
        pltpu.VMEM((ng, nc - 1, ci, LANES), BF),
        pltpu.VMEM((ng, nc - 1, nx, ci, LANES), BF),
        pltpu.VMEM((ng, nc - 1, nx, ci, LANES), BF),
        pltpu.VMEM((ng, nx - 1, ci, LANES), BF),
        pltpu.VMEM((ng, nx - 1, ci, LANES), BF),
        pltpu.VMEM((ng, nx, ci, LANES), F32),
        dma(()), dma((ax,)), dma(()),
        dma((2, nx, nc)), dma((2, nx, nc)),
        dma((2, nx, nc)), dma((2, nx, nc)),
        dma((2, nx, nc)), dma((2, nx, nc)),
        dma((nc,)), dma((nc,)),
        dma((ng,)), dma((ng,)),
        dma((ng, nx)), dma((ng, nx)),
        dma((ng, nc)), dma((ng, nc)),
    ]
    vmem = pl.BlockSpec(memory_space=pltpu.VMEM)
    hbm = pl.BlockSpec(memory_space=pltpu.HBM)
    sums = pl.pallas_call(
        functools.partial(kernel, ns, nc),
        out_shape=(
            jax.ShapeDtypeStruct(volume.shape, BF),
            jax.ShapeDtypeStruct((8, ci, oc), F32),
        ),
        in_specs=[hbm, hbm, hbm],
        out_specs=(vmem, vmem),
        scratch_shapes=scratch,
        compiler_params=pltpu.CompilerParams(
            collective_id=0, has_side_effects=True, vmem_limit_bytes=32 << 20
        ),
        name="conv_grads",
    )(*(pltpu.with_memory_space_constraint(v, pltpu.HBM) for v in (volume, weight, cotangent.transpose(0, 1, 3, 2))))
    return pl.pallas_call(
        place,
        out_shape=(
            jax.ShapeDtypeStruct(volume.shape, BF),
            jax.ShapeDtypeStruct((8, ci, oc), F32),
        ),
        in_specs=[vmem, vmem],
        out_specs=(hbm, hbm),
        scratch_shapes=[dma((2,))],
        compiler_params=pltpu.CompilerParams(vmem_limit_bytes=8 << 20),
        name="place",
    )(*sums)


def solution(mesh):
    return jax.shard_map(
        functools.partial(shards, mesh.shape["space"], mesh.shape["chan"]),
        mesh=mesh,
        in_specs=(
            P(("groups", "space"), "chan", None, None),
            P(None, "space", "chan"),
            P(("groups", "space"), None, None, "chan"),
        ),
        out_specs=(P(("groups", "space"), "chan", None, None), P("groups", "space", "chan")),
        check_vma=False,
    )
```
